32 devices in a mesh: dp: 2 (over z_hi), expert: 8 (over y, x, core), tensor: 2 (over z_lo).
Axes of the slice: x: 2, y: 2, z: 4 (z_hi: 2, z_lo: 2; z = z_hi * 2 + z_lo), core: 2. Of those that a mesh axis runs over, the one named last changes fastest.
Arguments:
- tokens: bfloat16 [2048, 2048], P(('dp', 'expert')), may hold values from -6 to 6
- expert_ids: int32 [2048, 8], P(('dp', 'expert')), may hold values from 0 to 15, all different within a row; in each aligned block of 64 rows (0 to 63, 64 to 127, ...) at most 64 rows name the same one
- weights: bfloat16 [2, 16, 768, 2048], P(None, 'expert', 'tensor'), may hold values from -0.125 to 0.125
- first_moment: bfloat16 [2, 16, 768, 2048], P('dp', 'expert', 'tensor'), may hold values from -6 to 6
- second_moment: bfloat16 [2, 16, 768, 2048], P('dp', 'expert', 'tensor'), may hold values from 1 to 100
- hidden_grad: bfloat16 [2, 16, 768, 1024], P('dp', 'expert', 'tensor'), may hold values from -6 to 6
- swap_list: int32 [4, 2], replicated, may hold values from 0 to 15, as said below
Outputs:
- hidden: bfloat16 [2, 16, 768, 1024], P('dp', 'expert', 'tensor')
- token_grad: bfloat16 [2048, 2048], P(('dp', 'expert', 'tensor'))
- new_weights: bfloat16 [2, 16, 768, 2048], P('dp', 'expert', 'tensor')
- new_first: bfloat16 [2, 16, 768, 2048], P('dp', 'expert', 'tensor')
- new_second: bfloat16 [2, 16, 768, 2048], P('dp', 'expert', 'tensor')
The draws below stay inside these ranges and needn't reach their ends.
Inputs may be any that keep to these rules, and one draw needn't show every extreme that they name: `expert_ids`: each row names 8 different experts. Within the rows of one quarter block of 64 rows no expert is named by more than 64 rows, a bound that some block reaches. `swap_list`: expert e is owned by index e // 2 of expert. The owners of the two experts of a row are 4 indices apart, and no owner appears in two rows.
All inputs are finite; a program needn't handle non-finite values.
Results may differ from the reference program's by a relative error of at most 0.0065.
Values may be sent and summed in bfloat16 or wider, within the bound.
No kernel may reach another device: no remote copies, remote signals or barrier semaphores. Data moves between devices by JAX's collectives and lax.ppermute only.
A program may use at most 192 MiB of HBM per device.

```python
import math
import jax
import jax.numpy as jnp
import numpy as np
from jax import lax

D = 2048
FF = 768
TOP = 8
EXP_DEV = 2
EXPERTS = 16
QTOK = 64
CAPQ = 64
SLOTS = 1024
TOKENS = 2048
REPLICAS = 2
MOVES = 4
N_DP = 2
N_EXPERT = 8
N_TENSOR = 2


def draw_swap_list(key, part):
    owners = EXPERTS // EXP_DEV
    lower_owner = jax.random.permutation(key, owners // 2)[:MOVES].astype(jnp.int32)
    local_slots = jax.random.randint(jax.random.fold_in(key, 1), (MOVES, 2), 0, EXP_DEV).astype(jnp.int32)
    flipped = jax.random.randint(jax.random.fold_in(key, 2), (MOVES,), 0, 2).astype(jnp.int32)
    lower_expert = lower_owner * EXP_DEV + local_slots[:, 0]
    upper_expert = (lower_owner + owners // 2) * EXP_DEV + local_slots[:, 1]
    first_expert = jnp.where(flipped == 1, upper_expert, lower_expert)
    second_expert = jnp.where(flipped == 1, lower_expert, upper_expert)
    return jnp.stack([first_expert, second_expert], axis=1).astype(jnp.int32)


def level_of(stream_key, extent, cuts, smallest, high):
    level = 1.0
    for axis_at, parts in cuts:
        draws = jax.random.uniform(jax.random.fold_in(jax.random.fold_in(stream_key, 6), axis_at), (parts,), jnp.float32, smallest / len(cuts), high / len(cuts))
        level = level * jnp.repeat(jnp.exp(draws), extent[axis_at] // parts).reshape((-1,) + (1,) * (len(extent) - 1 - axis_at))
    return level


def routed_block(rng, own, number, rows, count, top, bound, lean):
    sequence = jax.random.permutation(rng, count)
    packed, ordinary = shares(count, rows * top, bound, lean, True), shares(count, rows * top, bound, lean, False)
    places = jnp.arange(count)

    def named(tallies, rotation):
        used = int((tallies > 0).sum())
        fixed = max(1, used // 4)
        moved = fixed + (places - fixed + rotation * (used - fixed)) % max(1, count - fixed)
        return jnp.zeros((count,), jnp.int32).at[sequence[jnp.where(places < fixed, places, moved)]].set(jnp.asarray(tallies, jnp.int32))

    tallies = jnp.where(number % 4 == 0, named(packed, number // 4), named(ordinary, number - number // 4 - 1))
    mixed = jax.random.permutation(jax.random.fold_in(own, 3), count)
    source_of, receiver = mixed[0:count // 2 * 2:2], mixed[1:count // 2 * 2:2]
    room = jnp.minimum(tallies[source_of] - 1, bound - tallies[receiver]) // 2
    room = jnp.where((source_of == sequence[0]) | (receiver == sequence[0]) | (tallies[receiver] == 0), 0, jnp.maximum(room, 0))
    moved = jax.random.randint(jax.random.fold_in(own, 4), (count // 2,), 0, 1 << 20) % (room + 1)
    tallies = tallies.at[source_of].add(-moved).at[receiver].add(moved)
    members = jnp.searchsorted(jnp.cumsum(tallies), jnp.arange(rows * top), side="right").astype(jnp.int32)
    listing = members.reshape(top, rows).T
    listing = listing[jax.random.permutation(jax.random.fold_in(own, 1), rows)]
    rotation = jax.random.randint(jax.random.fold_in(own, 2), (rows, 1), 0, top)
    return jnp.take_along_axis(listing, (jnp.arange(top)[None, :] + rotation) % top, axis=1)


def shares(number_of, total, reach, slope, full):
    weights = [(1 << 20) // math.isqrt(grade ** slope) + 1 for grade in range(1, number_of + 1)]
    largest = reach if full else min(reach, max(-(-total // number_of), total * weights[0] // sum(weights)))
    least = 1 if total - largest >= number_of - 1 else 0
    counts, surplus = [largest] + [least] * (number_of - 1), total - largest - least * (number_of - 1)
    while surplus > 0:
        movable = [i for i in range(1, number_of) if counts[i] < largest] or [i for i in range(1, number_of) if counts[i] < reach]
        mass, remaining = sum([weights[i] for i in movable]), surplus
        for i in movable:
            addition = min(reach - counts[i], max(1, remaining * weights[i] // mass), surplus)
            counts[i] = counts[i] + addition
            surplus = surplus - addition
    return np.array(counts)


def centred(stream_key, shape, deviation, bound, split=(), kind=jnp.bfloat16):
    gain = level_of(stream_key, shape, split, -0.22, 0.18) if split else 1.0
    drawn = jax.random.normal(stream_key, shape, jnp.float32) * deviation * gain
    return jnp.minimum(jnp.maximum(drawn, -bound), bound).astype(kind)


def setup_inputs(seed: int = 0) -> dict:
    seeds = jax.random.split(jax.random.key(seed), 8)
    tokens = centred(seeds[0], (TOKENS, D), 1.0, 6.0, ((0, 16),))
    expert_ids_keys = jax.random.split(jax.random.fold_in(seeds[1], 1), TOKENS // QTOK)
    expert_ids_turns = jax.random.permutation(jax.random.fold_in(seeds[1], 3), TOKENS // QTOK)
    expert_ids = jax.vmap(lambda own, number: routed_block(jax.random.fold_in(seeds[1], 2), own, number, QTOK, EXPERTS, TOP, CAPQ, 2))(expert_ids_keys, expert_ids_turns).reshape((TOKENS, TOP))
    weights = centred(seeds[2], (2, EXPERTS, FF, D), D ** -0.5, 0.125, ((1, 8), (2, 2)))
    first_moment = centred(seeds[3], (2, EXPERTS, FF, D), 1.0, 6.0, ((0, 2), (1, 8), (2, 2)))
    second_moment = jnp.clip(jnp.exp(math.log(100.0) - 4.6051702 * jax.random.uniform(seeds[4], (2, EXPERTS, FF, D), jnp.float32) ** level_of(seeds[4], (2, EXPERTS, FF, D), ((0, 2), (1, 8), (2, 2)), -0.2, 0.2)), 1.0, 100.0).astype(jnp.bfloat16)
    hidden_grad = centred(seeds[5], (REPLICAS, EXPERTS, FF, SLOTS), 1.0, 6.0, ((0, 2), (1, 8), (2, 2)))
    swap_list = draw_swap_list(jax.random.fold_in(seeds[7], 71), 0)
    return {"tokens": tokens, "expert_ids": expert_ids, "weights": weights, "first_moment": first_moment, "second_moment": second_moment, "hidden_grad": hidden_grad, "swap_list": swap_list}


beta_one = 0.9
beta_two = 0.95
step_size = 0.01
adam_eps = 1e-08

def build_slot_map(expert_ids):
    blocks_total = N_DP * N_EXPERT * N_TENSOR
    pair_count = QTOK * TOP
    named_flat = expert_ids.reshape(blocks_total, pair_count)
    one_hot = (named_flat[:, :, None] == jnp.arange(EXPERTS, dtype=jnp.int32)[None, None, :]).astype(jnp.int32)
    slot_rank = lax.optimization_barrier(jnp.sum(jnp.cumsum(one_hot, axis=1) * one_hot, axis=2)) - 1
    block_index = jnp.arange(blocks_total, dtype=jnp.int32)[:, None]
    replica = block_index // (N_EXPERT * N_TENSOR)
    source = block_index % (N_EXPERT * N_TENSOR)
    pair_index = jnp.arange(pair_count, dtype=jnp.int32)[None, :]
    token_row = block_index * QTOK + pair_index // TOP
    slot_index = source * CAPQ + slot_rank
    replica_full = jnp.broadcast_to(replica, named_flat.shape)
    token_full = jnp.broadcast_to(token_row, named_flat.shape).astype(jnp.int32)
    empty_map = jnp.full((N_DP, EXPERTS, SLOTS), -1, jnp.int32)
    return empty_map.at[replica_full, named_flat, slot_index].set(token_full)

def reference(tokens, expert_ids, weights, first_moment, second_moment, hidden_grad, swap_list):
    slot_map = build_slot_map(expert_ids)
    shard_width = FF // N_TENSOR
    per_weight = jnp.moveaxis(weights, 1, 0)
    per_first = jnp.moveaxis(first_moment, 1, 0)
    per_second = jnp.moveaxis(second_moment, 1, 0)
    per_grad = jnp.moveaxis(hidden_grad, 1, 0)
    per_map = jnp.moveaxis(slot_map, 1, 0)

    def one_expert(running, inputs):
        weight, first, second, grad_hidden, owner = inputs
        filled = owner >= 0
        safe_owner = jnp.maximum(owner, 0)
        routed = jnp.where(filled[..., None], tokens[safe_owner], jnp.zeros((), jnp.bfloat16))
        routed_wide = routed.astype(jnp.float32)
        weight_wide = weight.astype(jnp.float32)
        projected = jnp.einsum('rsd,cfd->rscf', routed_wide, weight_wide)
        gate_pre = projected[:, :, 0]
        up_pre = projected[:, :, 1]
        sigmoid_gate = jax.nn.sigmoid(gate_pre)
        hidden = jnp.swapaxes((gate_pre * sigmoid_gate * up_pre).astype(jnp.bfloat16), 1, 2)
        grad_wide = jnp.swapaxes(grad_hidden, 1, 2).astype(jnp.float32)
        grad_gate = grad_wide * up_pre * sigmoid_gate * (1.0 + gate_pre * (1.0 - sigmoid_gate))
        grad_up = grad_wide * gate_pre * sigmoid_gate
        grad_pre = jnp.stack([grad_gate, grad_up], axis=2).astype(jnp.bfloat16)
        grad_pre_wide = grad_pre.astype(jnp.float32)
        summed = jnp.zeros((N_DP, SLOTS, D), jnp.float32)
        for shard_index in range(N_TENSOR):
            lower = shard_index * shard_width
            partial_term = jnp.einsum('rscf,cfd->rsd', grad_pre_wide[..., lower:lower + shard_width], weight_wide[:, lower:lower + shard_width, :])
            rounded = lax.optimization_barrier(partial_term.astype(jnp.bfloat16))
            summed = summed + rounded.astype(jnp.float32)
        slot_grad = lax.optimization_barrier(summed.astype(jnp.bfloat16))
        running = running.at[safe_owner].add(jnp.where(filled[..., None], slot_grad.astype(jnp.float32), jnp.float32(0.0)))
        weight_grad = jnp.einsum('rsd,rscf->cfd', routed_wide, grad_pre_wide)
        first_next = beta_one * first.astype(jnp.float32) + (1.0 - beta_one) * weight_grad
        second_next = beta_two * second.astype(jnp.float32) + (1.0 - beta_two) * weight_grad * weight_grad
        updated = weight_wide - step_size * first_next / (jnp.sqrt(second_next) + adam_eps)
        outputs = (hidden, updated.astype(jnp.bfloat16), first_next.astype(jnp.bfloat16), second_next.astype(jnp.bfloat16))
        return (running, outputs)
    start_grad = jnp.zeros((TOKENS, D), jnp.float32)
    running, stacked = lax.scan(one_expert, start_grad, (per_weight, per_first, per_second, per_grad, per_map))
    hidden_all, updated_all, first_all, second_all = stacked
    identity = jnp.arange(EXPERTS, dtype=jnp.int32)
    permuted = identity.at[swap_list[:, 0]].set(swap_list[:, 1]).at[swap_list[:, 1]].set(swap_list[:, 0])
    new_weights = jnp.moveaxis(jnp.take(updated_all, permuted, axis=0), 0, 1)
    new_first = jnp.moveaxis(jnp.take(first_all, permuted, axis=0), 0, 1)
    new_second = jnp.moveaxis(jnp.take(second_all, permuted, axis=0), 0, 1)
    hidden = jnp.moveaxis(hidden_all, 0, 1)
    return (hidden, running.astype(jnp.bfloat16), new_weights, new_first, new_second)
```

```python
import jax
import jax.numpy as jnp
from jax import lax
from jax.experimental import pallas as pl
from jax.experimental.pallas import tpu as pltpu
from jax.sharding import PartitionSpec as P

beta_one = 0.9
beta_two = 0.95
step_size = 0.01
adam_eps = 1e-08


def partner(value, axis, bit):
    return lax.ppermute(value, axis, [(i, i ^ 1 << bit) for i in range(lax.axis_size(axis))])


def slot_select(expert_ids, blocks, per_dev, owners, capacity):
    row_total = expert_ids.shape[0]
    top_count = expert_ids.shape[1]
    pair_total = row_total * top_count
    block_pairs = pair_total // blocks
    expert_total = per_dev * owners
    named_flat = expert_ids.reshape(blocks, block_pairs)
    one_hot = (
        named_flat[:, :, None] == jnp.arange(expert_total, dtype=jnp.int32)[None, None, :]
    ).astype(jnp.int32)
    slot_rank = (jnp.sum(jnp.cumsum(one_hot, axis=1) * one_hot, axis=2) - 1).reshape(pair_total)
    block_index = jnp.arange(pair_total, dtype=jnp.int32) // block_pairs
    expert_flat = named_flat.reshape(pair_total)
    slot_key = (
        (expert_flat % per_dev * owners + expert_flat // per_dev) * blocks + block_index
    ) * capacity + slot_rank
    key_total = expert_total * blocks * capacity
    by_key = (jnp.arange(key_total, dtype=jnp.int32)[:, None] == slot_key[None, :]).astype(
        jnp.bfloat16
    )
    pair_rows = jnp.arange(pair_total, dtype=jnp.int32) // top_count
    by_row = (pair_rows[:, None] == jnp.arange(row_total, dtype=jnp.int32)[None, :]).astype(
        jnp.bfloat16
    )
    return jnp.dot(by_key, by_row, preferred_element_type=jnp.float32).astype(jnp.bfloat16)


def migration_slot(swap_list, per_dev):
    own_index = lax.axis_index("expert")
    first_hit = swap_list[:, 0] // per_dev == own_index
    second_hit = swap_list[:, 1] // per_dev == own_index
    chosen = jnp.sum(
        jnp.where(first_hit, swap_list[:, 0] % per_dev, 0)
        + jnp.where(second_hit, swap_list[:, 1] % per_dev, 0)
    )
    return (chosen, jnp.any(first_hit | second_hit))


def pick_slot(state, chosen):
    return lax.dynamic_index_in_dim(state, chosen, 1, keepdims=False)


def place_slot(state, incoming, chosen, moving):
    target = (jnp.arange(state.shape[1], dtype=jnp.int32) == chosen) & moving
    return jnp.where(target[None, :, None, None], incoming[:, None], state)


def adam_step(weight_half, first_moment, second_moment, weight_grad):
    first_next = beta_one * first_moment.astype(jnp.float32) + (1.0 - beta_one) * weight_grad
    second_next = (
        beta_two * second_moment.astype(jnp.float32) + (1.0 - beta_two) * weight_grad * weight_grad
    )
    updated = weight_half.astype(jnp.float32) - step_size * first_next / (
        jnp.sqrt(second_next) + adam_eps
    )
    return (
        updated.astype(jnp.bfloat16),
        first_next.astype(jnp.bfloat16),
        second_next.astype(jnp.bfloat16),
    )


def shards(tokens, expert_ids, weights, first_moment, second_moment, hidden_grad, swap_list):
    owners = lax.axis_size("expert")
    tensor_count = lax.axis_size("tensor")
    replicas = lax.axis_size("dp")
    per_dev = weights.shape[1]
    model_width = tokens.shape[1]
    slots_total = hidden_grad.shape[3]
    capacity = slots_total // (owners * tensor_count)
    quarter_rows = tokens.shape[0] // tensor_count
    quarter_index = lax.axis_index("tensor")
    whole_select = slot_select(expert_ids, tensor_count, per_dev, owners, capacity)
    outgoing = jnp.dot(whole_select, tokens, preferred_element_type=jnp.float32).astype(
        jnp.bfloat16
    )
    outgoing = outgoing.reshape(per_dev, owners, tensor_count * capacity, model_width)
    arrived = lax.all_to_all(outgoing, "expert", split_axis=1, concat_axis=1, tiled=True)
    select_grid = whole_select.reshape(
        per_dev, owners, tensor_count, capacity, tensor_count, quarter_rows
    )
    select_grid = lax.dynamic_index_in_dim(select_grid, quarter_index, 2, keepdims=False)
    select_grid = lax.dynamic_index_in_dim(select_grid, quarter_index, 3, keepdims=False)
    own_select = select_grid.reshape(per_dev * owners * capacity, quarter_rows)
    routed = arrived.reshape(per_dev, slots_total, model_width)
    half_rows = 2 // replicas
    replica_index = lax.axis_index("dp")
    weight_half = lax.dynamic_slice_in_dim(weights, replica_index * half_rows, half_rows, 0)
    chosen, moving = migration_slot(swap_list, per_dev)
    top_bit = owners.bit_length() - 2
    projected = jnp.einsum("cefd,esd->ecfs", weights, routed, preferred_element_type=jnp.float32)
    gate_pre = projected[:, 0]
    up_pre = projected[:, 1]
    sigmoid_gate = jax.nn.sigmoid(gate_pre)
    hidden = (gate_pre * sigmoid_gate * up_pre).astype(jnp.bfloat16)
    grad_hidden = hidden_grad[0].astype(jnp.float32)
    grad_gate = grad_hidden * up_pre * sigmoid_gate * (1.0 + gate_pre * (1.0 - sigmoid_gate))
    grad_up = grad_hidden * gate_pre * sigmoid_gate
    grad_pre = jnp.stack([grad_gate, grad_up], axis=1).astype(jnp.bfloat16)
    slot_terms = jnp.einsum("ecfs,cefd->esd", grad_pre, weights, preferred_element_type=jnp.float32)
    slot_terms = slot_terms.reshape(per_dev, owners, tensor_count, capacity, model_width)
    summed = lax.psum_scatter(
        slot_terms.astype(jnp.bfloat16), "tensor", scatter_dimension=2, tiled=True
    )
    returning = summed.reshape(per_dev, owners, capacity, model_width)
    back_rows = lax.all_to_all(returning, "expert", split_axis=1, concat_axis=1, tiled=True)
    token_grad = jnp.dot(
        own_select.T,
        back_rows.reshape(per_dev * owners * capacity, model_width),
        preferred_element_type=jnp.float32,
    ).astype(jnp.bfloat16)

    def grad_rows(offset, number):
        part_grad = lax.dynamic_slice_in_dim(grad_pre, offset, number, 1)
        return jnp.einsum("esd,ecfs->cefd", routed, part_grad, preferred_element_type=jnp.float32)

    own_term = grad_rows(replica_index * half_rows, half_rows)
    other_term = grad_rows((1 - replica_index) * half_rows, half_rows)
    weight_grad = own_term + partner(other_term, "dp", 0)
    updated, first_next, second_next = adam_step(
        weight_half, first_moment, second_moment, weight_grad
    )
    arrived_states = partner(
        (pick_slot(updated, chosen), pick_slot(first_next, chosen), pick_slot(second_next, chosen)),
        "expert",
        top_bit,
    )
    new_weights = place_slot(updated, arrived_states[0], chosen, moving)
    new_first = place_slot(first_next, arrived_states[1], chosen, moving)
    new_second = place_slot(second_next, arrived_states[2], chosen, moving)
    return (hidden[None], token_grad, new_weights, new_first, new_second)


IDS_COLS = 128
CORE, X_BIT, Y_BIT = 1, 2, 4


def flip(value, axis, mask):
    return lax.ppermute(value, axis, [(i, i ^ mask) for i in range(lax.axis_size(axis))])


def after(value, *others):
    return lax.optimization_barrier((value, *others))[0]


def gather_chips(rows):
    half = rows.shape[0] // 2
    low, high = rows[:half], rows[half:]
    low_y = flip(low, "expert", Y_BIT)
    high_x = flip(high, "expert", X_BIT)
    low_x = flip(jnp.concatenate([low, low_y]), "expert", X_BIT)
    high_y = flip(jnp.concatenate([high, high_x]), "expert", Y_BIT)
    return jnp.concatenate(
        [low, high, low_x[:half], high_x, low_y, high_y[:half], low_x[half:], high_y[half:]]
    )


def select_rows(ids, expert, core):
    rows = ids.shape[0]
    quarter = rows // 4
    row = lax.broadcasted_iota(jnp.int32, (rows, rows), 0)
    col = lax.broadcasted_iota(jnp.int32, (rows, rows), 1)
    earlier = ((row // quarter == col // quarter) & (col < row)).astype(jnp.bfloat16)
    hit = jnp.sum(jnp.where(ids == expert.astype(jnp.float32), 1.0, 0.0), axis=1, keepdims=True)
    hit = jnp.broadcast_to(hit, (rows, rows))
    rank = jnp.dot(earlier, hit.astype(jnp.bfloat16), preferred_element_type=jnp.float32)
    part = row // (rows // 2)
    owner = jnp.where(core == 0, part, 1 - part)
    base = owner * (rows // 2) + (row % (rows // 2)) // quarter * quarter
    taken = (rank.astype(jnp.int32) + base == col) & (hit > 0.5)
    return jnp.where(taken, 1.0, 0.0).astype(jnp.bfloat16)


def dot_nt(a, b):
    return lax.dot_general(a, b, (((1,), (1,)), ((), ())), preferred_element_type=jnp.float32)


def dot_tn(a, b):
    return lax.dot_general(a, b, (((0,), (0,)), ((), ())), preferred_element_type=jnp.float32)


def block_rows(a_ref, b_ref, width):
    rows = jnp.concatenate([a_ref[0], b_ref[0]], axis=0)
    return rows[:, :width], rows[:, width:].astype(jnp.float32)


def gradients(gate, up, grad):
    sig = jax.nn.sigmoid(gate)
    grad_gate = grad * up * sig * (1.0 + gate * (1.0 - sig))
    grad_up = grad * gate * sig
    return sig, grad_gate, grad_up


def own_kernel(info, a_ref, b_ref, w_ref, hg_ref, hidden_ref, grad_ref, ta_ref, tb_ref):
    core, base, replica = info[1], info[3], info[4]
    width = w_ref.shape[3]
    rows, ids = block_rows(a_ref, b_ref, width)
    half = rows.shape[0] // 2
    total = None
    for e in range(w_ref.shape[1]):
        select = select_rows(ids, base + e, core)
        gate = dot_nt(w_ref[0, e], rows)
        up = dot_nt(w_ref[1, e], rows)
        grad = dot_nt(hg_ref[0, e], select)
        sig, grad_gate, grad_up = gradients(gate, up, grad)
        hidden = (gate * sig * up).astype(jnp.bfloat16)
        hidden_ref[0, e] = jnp.dot(hidden, select, preferred_element_type=jnp.float32).astype(
            jnp.bfloat16
        )
        chosen = jnp.where(replica == 0, grad_gate, grad_up).astype(jnp.bfloat16)
        grad_ref[e, 0] = chosen[:, :half]
        grad_ref[e, 1] = chosen[:, half:]
        term = dot_tn(grad_gate.astype(jnp.bfloat16), w_ref[0, e])
        term = term + dot_tn(grad_up.astype(jnp.bfloat16), w_ref[1, e])
        total = term if total is None else total + term
    total = total.astype(jnp.bfloat16)
    ta_ref[0] = total[:half]
    tb_ref[0] = total[half:]


def other_kernel(info, a_ref, b_ref, w_ref, hg_ref, grad_ref):
    expert, core, base, replica = info[0], info[1], info[3], info[4]
    width = w_ref.shape[3]
    rows, ids = block_rows(a_ref, b_ref, width)
    half = rows.shape[0] // 2
    select = select_rows(ids, base + expert, core)
    gate = dot_nt(w_ref[0, 0], rows)
    up = dot_nt(w_ref[1, 0], rows)
    grad = dot_nt(hg_ref[...], select)
    _, grad_gate, grad_up = gradients(gate, up, grad)
    chosen = jnp.where(replica == 0, grad_gate, grad_up).astype(jnp.bfloat16)
    grad_ref[0] = chosen[:, :half]
    grad_ref[1] = chosen[:, half:]


def weight_gradient(own_ref, other_ref, tokens):
    a_ref, b_ref, c_ref, d_ref = tokens
    return (
        jnp.dot(own_ref[0, 0], a_ref[...], preferred_element_type=jnp.float32)
        + jnp.dot(own_ref[0, 1], b_ref[...], preferred_element_type=jnp.float32)
        + jnp.dot(other_ref[0], c_ref[...], preferred_element_type=jnp.float32)
        + jnp.dot(other_ref[1], d_ref[...], preferred_element_type=jnp.float32)
    )


def moments(grad, first, second):
    first = beta_one * first.astype(jnp.float32) + (1.0 - beta_one) * grad
    second = beta_two * second.astype(jnp.float32) + (1.0 - beta_two) * grad * grad
    return first, second


def step_weights(weight, first, second):
    return weight.astype(jnp.float32) - step_size * first / (jnp.sqrt(second) + adam_eps)


def leaving_kernel(info, own, other, a, b, c, d, m_ref, v_ref, first_ref, second_ref):
    grad = weight_gradient(own, other, (a, b, c, d))
    first, second = moments(grad, m_ref[0, 0], v_ref[0, 0])
    first_ref[...] = first.astype(jnp.bfloat16)
    second_ref[...] = second.astype(jnp.bfloat16)


def staying_kernel(info, own, other, a, b, c, d, m_ref, v_ref, w_ref, nw_ref, nm_ref, nv_ref):
    grad = weight_gradient(own, other, (a, b, c, d))
    first, second = moments(grad, m_ref[0, 0], v_ref[0, 0])
    nw_ref[0, 0] = step_weights(w_ref[0, 0], first, second).astype(jnp.bfloat16)
    nm_ref[0, 0] = first.astype(jnp.bfloat16)
    nv_ref[0, 0] = second.astype(jnp.bfloat16)


def arriving_kernel(info, _w, _m, _v, w_ref, m_ref, v_ref, nw_ref, nm_ref, nv_ref):
    first, second = m_ref[...], v_ref[...]
    nw_ref[0, 0] = step_weights(
        w_ref[...], first.astype(jnp.float32), second.astype(jnp.float32)
    ).astype(jnp.bfloat16)
    nm_ref[0, 0] = first
    nv_ref[0, 0] = second


def call(kernel, grid, in_specs, out_specs, out_shape, flops, bytes_accessed, **extra):
    return pl.pallas_call(
        kernel,
        grid_spec=pltpu.PrefetchScalarGridSpec(
            num_scalar_prefetch=1, grid=grid, in_specs=in_specs, out_specs=out_specs
        ),
        out_shape=out_shape,
        cost_estimate=pl.CostEstimate(
            flops=flops, bytes_accessed=bytes_accessed, transcendentals=0
        ),
        **extra,
    )


def fast_shards(tokens, expert_ids, weights, first_moment, second_moment, hidden_grad, swap_list):
    owners = lax.axis_size("expert")
    row_count, width = tokens.shape
    _, per_dev, hidden_units, slots_total = hidden_grad.shape
    chips = owners // 2
    bf16 = jnp.bfloat16
    replica = lax.axis_index("dp")
    own_index = lax.axis_index("expert")
    quarter = lax.axis_index("tensor")
    chosen, _ = migration_slot(swap_list, per_dev)
    staying = 1 - chosen
    core, chip, base = own_index % 2, own_index // 2, own_index * per_dev
    info_leave = jnp.stack([chosen, core, chip, base, replica]).astype(jnp.int32)
    info_stay = jnp.stack([staying, core, chip, base, replica]).astype(jnp.int32)

    ids = jnp.pad(
        expert_ids.astype(bf16), ((0, 0), (0, IDS_COLS - expert_ids.shape[1])), constant_values=-1
    )
    rows = jnp.concatenate([tokens, ids], axis=1)
    own_a = gather_chips(rows)
    own_b = flip(own_a, "expert", CORE)
    crossed = flip(rows, "dp", 1)
    other_a = gather_chips(crossed)
    other_b = flip(other_a, "expert", CORE)

    leave_grad = lax.dynamic_index_in_dim(hidden_grad[0], chosen, 0, keepdims=False)
    stay_grad = lax.dynamic_index_in_dim(hidden_grad[0], staying, 0, keepdims=False)
    leave_other = flip(after(leave_grad, crossed), "dp", 1)
    stay_other = flip(after(stay_grad, leave_other), "dp", 1)

    weight_half = lax.dynamic_index_in_dim(weights, replica, 0, keepdims=False)
    leave_weight = lax.dynamic_index_in_dim(weight_half, chosen, 0, keepdims=False)
    new_weight_in = flip(after(leave_weight, own_a), "expert", Y_BIT)

    wide = rows.shape[1]
    blocks = lambda value: value.reshape(chips, row_count, wide)
    token_spec = pl.BlockSpec((1, row_count, wide), lambda k, info: (k, 0, 0))
    at_chip = lambda k, info: jnp.bitwise_xor(info[2], k)
    pair = 2 * row_count
    matmul = 2 * per_dev * hidden_units * width * chips * pair * 2
    hidden, own_grad, ta, tb = call(
        own_kernel,
        (chips,),
        [
            token_spec,
            token_spec,
            pl.BlockSpec(weights.shape, lambda k, info: (0, 0, 0, 0), pipeline_mode=pl.Buffered(1)),
            pl.BlockSpec(
                (1, per_dev, hidden_units, pair), lambda k, info: (0, 0, 0, at_chip(k, info))
            ),
        ],
        [
            pl.BlockSpec(
                (1, per_dev, hidden_units, pair), lambda k, info: (0, 0, 0, at_chip(k, info))
            ),
            pl.BlockSpec((per_dev, 2, hidden_units, row_count), lambda k, info: (0, 0, 0, k)),
            pl.BlockSpec((1, row_count, width), lambda k, info: (k, 0, 0)),
            pl.BlockSpec((1, row_count, width), lambda k, info: (k, 0, 0)),
        ],
        [
            jax.ShapeDtypeStruct(hidden_grad.shape, bf16),
            jax.ShapeDtypeStruct((per_dev, 2, hidden_units, chips * row_count), bf16),
            jax.ShapeDtypeStruct((chips, row_count, width), bf16),
            jax.ShapeDtypeStruct((chips, row_count, width), bf16),
        ],
        2 * matmul,
        20 << 20,
    )(info_leave, blocks(own_a), blocks(own_b), weights, hidden_grad)

    def other_grad(info, grad):
        return call(
            other_kernel,
            (chips,),
            [
                token_spec,
                token_spec,
                pl.BlockSpec(
                    (2, 1, hidden_units, width),
                    lambda k, info: (0, info[0], 0, 0),
                    pipeline_mode=pl.Buffered(1),
                ),
                pl.BlockSpec((hidden_units, pair), lambda k, info: (0, at_chip(k, info))),
            ],
            pl.BlockSpec((2, hidden_units, row_count), lambda k, info: (0, 0, k)),
            jax.ShapeDtypeStruct((2, hidden_units, chips * row_count), bf16),
            matmul // 2,
            9 << 20,
        )(info, blocks(other_a), blocks(other_b), weights, grad)

    tile = 256
    tiles = width // tile
    flat_rows = chips * row_count
    flat_spec = pl.BlockSpec((flat_rows, tile), lambda j, info: (0, j))
    state_spec = pl.BlockSpec(
        (1, 1, hidden_units, tile), lambda j, info: (0, info[0], 0, j)
    )
    grad_specs = [
        pl.BlockSpec((1, 2, hidden_units, flat_rows), lambda j, info: (info[0], 0, 0, 0)),
        pl.BlockSpec((2, hidden_units, flat_rows), lambda j, info: (0, 0, 0)),
        flat_spec,
        flat_spec,
        flat_spec,
        flat_spec,
    ]
    plain_spec = pl.BlockSpec((hidden_units, tile), lambda j, info: (0, j))
    plain_shape = jax.ShapeDtypeStruct((hidden_units, width), bf16)
    leave_first, leave_second = call(
        leaving_kernel,
        (tiles,),
        grad_specs + [state_spec, state_spec],
        [plain_spec, plain_spec],
        [plain_shape, plain_shape],
        matmul // 2,
        18 << 20,
    )(
        info_leave,
        own_grad,
        other_grad(info_leave, leave_other),
        own_a,
        own_b,
        other_a,
        other_b,
        first_moment,
        second_moment,
    )
    second_in = flip(leave_second, "expert", Y_BIT)
    first_in = flip(leave_first, "expert", Y_BIT)

    state_shape = jax.ShapeDtypeStruct(first_moment.shape, bf16)
    stay_states = call(
        staying_kernel,
        (tiles,),
        grad_specs
        + [
            state_spec,
            state_spec,
            pl.BlockSpec((1, 1, hidden_units, tile), lambda j, info: (info[4], info[0], 0, j)),
        ],
        [state_spec] * 3,
        [state_shape] * 3,
        matmul // 2,
        20 << 20,
    )(
        info_stay,
        own_grad,
        other_grad(info_stay, stay_other),
        own_a,
        own_b,
        other_a,
        other_b,
        first_moment,
        second_moment,
        weights,
    )

    f32 = jnp.float32
    core_sum = ta.astype(f32) + flip(tb, "expert", CORE).astype(f32)
    core_sum = core_sum.reshape(2, 2, row_count, width)
    x_sum = core_sum[:, 0] + flip(core_sum[:, 1].astype(bf16), "expert", X_BIT).astype(f32)
    x_sum = x_sum.reshape(2, 2, row_count // 2, width)
    mine = lax.dynamic_index_in_dim(x_sum, quarter, 1, keepdims=False)
    theirs = lax.dynamic_index_in_dim(x_sum, 1 - quarter, 1, keepdims=False)
    z_sum = mine + flip(theirs.astype(bf16), "tensor", 1).astype(f32)
    token_grad = z_sum[0] + flip(z_sum[1].astype(bf16), "expert", Y_BIT).astype(f32)

    row_tile = 128
    any_spec = pl.BlockSpec(memory_space=pl.ANY)
    in_spec = pl.BlockSpec((row_tile, width), lambda i, info: (i, 0))
    out_spec = pl.BlockSpec((1, 1, row_tile, width), lambda i, info: (0, info[0], i, 0))
    new_weights, new_first, new_second = call(
        arriving_kernel,
        (hidden_units // row_tile,),
        [any_spec] * 3 + [in_spec] * 3,
        [out_spec] * 3,
        [state_shape] * 3,
        0,
        9 << 20,
        input_output_aliases={1: 0, 2: 1, 3: 2},
    )(info_leave, *stay_states, new_weight_in, first_in, second_in)
    return (hidden, token_grad.astype(bf16), new_weights, new_first, new_second)


def token_layout_fits(tokens, expert_ids, weights, first, second, hidden_grad, swap_list):
    owners, parts = lax.axis_size("expert"), lax.axis_size("tensor")
    return (
        lax.axis_size("dp") == 2
        and owners == 8
        and parts == 2
        and weights.shape[1] == 2
        and 2 * swap_list.shape[0] == owners
        and tokens.shape[0] == 128
        and hidden_grad.shape[3] == owners * tokens.shape[0]
        and weights.shape[2] % 128 == 0
        and tokens.shape[1] % 256 == 0
    )


def plan(*args):
    return fast_shards(*args) if token_layout_fits(*args) else shards(*args)


def solution(mesh):
    in_specs = (
        P(("dp", "expert"), None),
        P(("dp", "expert"), None),
        P(None, "expert", "tensor", None),
        P("dp", "expert", "tensor", None),
        P("dp", "expert", "tensor", None),
        P("dp", "expert", "tensor", None),
        P(),
    )
    out_specs = (
        P("dp", "expert", "tensor", None),
        P(("dp", "expert", "tensor"), None),
        P("dp", "expert", "tensor", None),
        P("dp", "expert", "tensor", None),
        P("dp", "expert", "tensor", None),
    )
    return jax.shard_map(plan, mesh=mesh, in_specs=in_specs, out_specs=out_specs, check_vma=False)
```

```python
import jax
import jax.numpy as jnp
from jax import lax
from jax.experimental import pallas as pl
from jax.experimental.pallas import tpu as pltpu
from jax.sharding import PartitionSpec as P


beta_one = 0.9
beta_two = 0.95
step_size = 0.01
adam_eps = 1e-08


def partner(value, axis, bit):
    return lax.ppermute(value, axis, [(i, i ^ 1 << bit) for i in range(lax.axis_size(axis))])


def slot_select(expert_ids, blocks, per_dev, owners, capacity):
    row_total = expert_ids.shape[0]
    top_count = expert_ids.shape[1]
    pair_total = row_total * top_count
    block_pairs = pair_total // blocks
    expert_total = per_dev * owners
    named_flat = expert_ids.reshape(blocks, block_pairs)
    one_hot = (
        named_flat[:, :, None] == jnp.arange(expert_total, dtype=jnp.int32)[None, None, :]
    ).astype(jnp.int32)
    slot_rank = (jnp.sum(jnp.cumsum(one_hot, axis=1) * one_hot, axis=2) - 1).reshape(pair_total)
    block_index = jnp.arange(pair_total, dtype=jnp.int32) // block_pairs
    expert_flat = named_flat.reshape(pair_total)
    slot_key = (
        (expert_flat % per_dev * owners + expert_flat // per_dev) * blocks + block_index
    ) * capacity + slot_rank
    key_total = expert_total * blocks * capacity
    by_key = (jnp.arange(key_total, dtype=jnp.int32)[:, None] == slot_key[None, :]).astype(
        jnp.bfloat16
    )
    pair_rows = jnp.arange(pair_total, dtype=jnp.int32) // top_count
    by_row = (pair_rows[:, None] == jnp.arange(row_total, dtype=jnp.int32)[None, :]).astype(
        jnp.bfloat16
    )
    return jnp.dot(by_key, by_row, preferred_element_type=jnp.float32).astype(jnp.bfloat16)


def migration_slot(swap_list, per_dev):
    own_index = lax.axis_index("expert")
    first_hit = swap_list[:, 0] // per_dev == own_index
    second_hit = swap_list[:, 1] // per_dev == own_index
    chosen = jnp.sum(
        jnp.where(first_hit, swap_list[:, 0] % per_dev, 0)
        + jnp.where(second_hit, swap_list[:, 1] % per_dev, 0)
    )
    return (chosen, jnp.any(first_hit | second_hit))


def pick_slot(state, chosen):
    return lax.dynamic_index_in_dim(state, chosen, 1, keepdims=False)


def place_slot(state, incoming, chosen, moving):
    target = (jnp.arange(state.shape[1], dtype=jnp.int32) == chosen) & moving
    return jnp.where(target[None, :, None, None], incoming[:, None], state)


def adam_step(weight_half, first_moment, second_moment, weight_grad):
    first_next = beta_one * first_moment.astype(jnp.float32) + (1.0 - beta_one) * weight_grad
    second_next = (
        beta_two * second_moment.astype(jnp.float32) + (1.0 - beta_two) * weight_grad * weight_grad
    )
    updated = weight_half.astype(jnp.float32) - step_size * first_next / (
        jnp.sqrt(second_next) + adam_eps
    )
    return (
        updated.astype(jnp.bfloat16),
        first_next.astype(jnp.bfloat16),
        second_next.astype(jnp.bfloat16),
    )


def shards(tokens, expert_ids, weights, first_moment, second_moment, hidden_grad, swap_list):
    owners = lax.axis_size("expert")
    tensor_count = lax.axis_size("tensor")
    replicas = lax.axis_size("dp")
    per_dev = weights.shape[1]
    model_width = tokens.shape[1]
    slots_total = hidden_grad.shape[3]
    capacity = slots_total // (owners * tensor_count)
    quarter_rows = tokens.shape[0] // tensor_count
    quarter_index = lax.axis_index("tensor")
    whole_select = slot_select(expert_ids, tensor_count, per_dev, owners, capacity)
    outgoing = jnp.dot(whole_select, tokens, preferred_element_type=jnp.float32).astype(
        jnp.bfloat16
    )
    outgoing = outgoing.reshape(per_dev, owners, tensor_count * capacity, model_width)
    arrived = lax.all_to_all(outgoing, "expert", split_axis=1, concat_axis=1, tiled=True)
    select_grid = whole_select.reshape(
        per_dev, owners, tensor_count, capacity, tensor_count, quarter_rows
    )
    select_grid = lax.dynamic_index_in_dim(select_grid, quarter_index, 2, keepdims=False)
    select_grid = lax.dynamic_index_in_dim(select_grid, quarter_index, 3, keepdims=False)
    own_select = select_grid.reshape(per_dev * owners * capacity, quarter_rows)
    routed = arrived.reshape(per_dev, slots_total, model_width)
    half_rows = 2 // replicas
    replica_index = lax.axis_index("dp")
    weight_half = lax.dynamic_slice_in_dim(weights, replica_index * half_rows, half_rows, 0)
    chosen, moving = migration_slot(swap_list, per_dev)
    top_bit = owners.bit_length() - 2
    projected = jnp.einsum("cefd,esd->ecfs", weights, routed, preferred_element_type=jnp.float32)
    gate_pre = projected[:, 0]
    up_pre = projected[:, 1]
    sigmoid_gate = jax.nn.sigmoid(gate_pre)
    hidden = (gate_pre * sigmoid_gate * up_pre).astype(jnp.bfloat16)
    grad_hidden = hidden_grad[0].astype(jnp.float32)
    grad_gate = grad_hidden * up_pre * sigmoid_gate * (1.0 + gate_pre * (1.0 - sigmoid_gate))
    grad_up = grad_hidden * gate_pre * sigmoid_gate
    grad_pre = jnp.stack([grad_gate, grad_up], axis=1).astype(jnp.bfloat16)
    slot_terms = jnp.einsum("ecfs,cefd->esd", grad_pre, weights, preferred_element_type=jnp.float32)
    slot_terms = slot_terms.reshape(per_dev, owners, tensor_count, capacity, model_width)
    summed = lax.psum_scatter(
        slot_terms.astype(jnp.bfloat16), "tensor", scatter_dimension=2, tiled=True
    )
    returning = summed.reshape(per_dev, owners, capacity, model_width)
    back_rows = lax.all_to_all(returning, "expert", split_axis=1, concat_axis=1, tiled=True)
    token_grad = jnp.dot(
        own_select.T,
        back_rows.reshape(per_dev * owners * capacity, model_width),
        preferred_element_type=jnp.float32,
    ).astype(jnp.bfloat16)

    def grad_rows(offset, number):
        part_grad = lax.dynamic_slice_in_dim(grad_pre, offset, number, 1)
        return jnp.einsum("esd,ecfs->cefd", routed, part_grad, preferred_element_type=jnp.float32)

    own_term = grad_rows(replica_index * half_rows, half_rows)
    other_term = grad_rows((1 - replica_index) * half_rows, half_rows)
    weight_grad = own_term + partner(other_term, "dp", 0)
    updated, first_next, second_next = adam_step(
        weight_half, first_moment, second_moment, weight_grad
    )
    arrived_states = partner(
        (pick_slot(updated, chosen), pick_slot(first_next, chosen), pick_slot(second_next, chosen)),
        "expert",
        top_bit,
    )
    new_weights = place_slot(updated, arrived_states[0], chosen, moving)
    new_first = place_slot(first_next, arrived_states[1], chosen, moving)
    new_second = place_slot(second_next, arrived_states[2], chosen, moving)
    return (hidden[None], token_grad, new_weights, new_first, new_second)


IDS_COLS = 128
VMEM_GRANT = 26 << 20
STAY_GRANT = 48 << 20
CORE, X_BIT, Y_BIT = 1, 2, 4
DP, EXPERT, TENSOR = "dp", "expert", "tensor"


def flip(value, axis, mask):
    return lax.ppermute(value, axis, [(i, i ^ mask) for i in range(lax.axis_size(axis))])


def after(value, *others):
    return lax.optimization_barrier((value, *others))[0]


def gather_chips(rows, direct=False, early=()):
    by_y = flip(rows, EXPERT, Y_BIT)
    by_x = flip(rows, EXPERT, X_BIT)
    if direct:
        by_xy = flip(rows, EXPERT, X_BIT | Y_BIT)
    else:
        by_xy = flip(after(by_y, *early), EXPERT, X_BIT)
    return [rows, by_x, by_y, by_xy]


def gather_plane(columns):
    result = []
    for k in range(len(columns[0])):
        mine = [chips[k] for chips in columns]
        result.append(mine + [flip(p, EXPERT, CORE) for p in mine])
    return result


def select_rows(ids, expert, core, turned):
    rows = ids.shape[0]
    shift = (rows // 4).bit_length() - 1
    row = lax.broadcasted_iota(jnp.int32, (rows, rows), 0)
    col = lax.broadcasted_iota(jnp.int32, (rows, rows), 1)
    quarter = row >> shift
    earlier = jnp.where((quarter == (col >> shift)) & (col < row), 1.0, 0.0).astype(jnp.bfloat16)
    hit = jnp.sum(jnp.where(ids == expert.astype(jnp.float32), 1.0, 0.0), axis=1, keepdims=True)
    hit = jnp.broadcast_to(hit, (rows, rows))
    rank = jnp.dot(earlier, hit.astype(jnp.bfloat16), preferred_element_type=jnp.float32)
    base = (quarter ^ (core * 2 + turned)) << shift
    taken = (rank.astype(jnp.int32) + base == col) & (hit > 0.5)
    return jnp.where(taken, 1.0, 0.0).astype(jnp.bfloat16)


def dot_nt(a, b):
    return lax.dot_general(a, b, (((1,), (1,)), ((), ())), preferred_element_type=jnp.float32)


def dot_tn(a, b):
    return lax.dot_general(a, b, (((0,), (0,)), ((), ())), preferred_element_type=jnp.float32)


def split_rows(rows, width):
    return rows[:, :width], rows[:, width:].astype(jnp.float32)


def take_pieces(pieces, buffer, sems):
    k, steps = pl.program_id(0), len(pieces)

    def copies(chip, slot):
        result, start = [], 0
        for i, piece in enumerate(pieces[chip]):
            where = buffer.at[slot, pl.ds(start, piece.shape[0])]
            result.append(pltpu.make_async_copy(piece, where, sems.at[slot, i]))
            start += piece.shape[0]
        return result

    for j in range(steps):

        @pl.when(k == j)
        def _(j=j):
            if j == 0:
                for copy in copies(0, 0):
                    copy.start()
            if j + 1 < steps:
                for copy in copies(j + 1, (j + 1) % 2):
                    copy.start()
            for copy in copies(j, j % 2):
                copy.wait()

    return buffer[k % 2]


def gradients(gate, up, grad):
    sig = jax.nn.sigmoid(gate)
    grad_gate = grad * up * sig * (1.0 + gate * (1.0 - sig))
    grad_up = grad * gate * sig
    return sig, grad_gate, grad_up


def own_kernel(pieces, info, w_ref, hg_ref, hidden_ref, grad_ref, rows_ref, buffer, sems):
    core, base = info[2], info[4]
    width = w_ref.shape[3]
    rows_ref[...] = take_pieces(pieces, buffer, sems)
    rows, ids = split_rows(rows_ref[...], width)
    per_dev, units = w_ref.shape[1], w_ref.shape[2]
    projected = dot_nt(w_ref[...].reshape(2 * per_dev * units, width), rows)
    projected = projected.reshape(2, per_dev, units, rows.shape[0])
    for e in range(per_dev):
        select = select_rows(ids, base + e, core, 0)
        gate, up = projected[0, e], projected[1, e]
        grad = dot_nt(hg_ref[0, e], select)
        sig, grad_gate, grad_up = gradients(gate, up, grad)
        hidden = (gate * sig * up).astype(jnp.bfloat16)
        hidden_ref[0, e] = jnp.dot(hidden, select, preferred_element_type=jnp.float32).astype(
            jnp.bfloat16
        )
        grad_ref[0, e] = grad_gate.astype(jnp.bfloat16)
        grad_ref[1, e] = grad_up.astype(jnp.bfloat16)


def token_kernel(info, grad_ref, w_ref, ta_ref, tb_ref):
    grad, weight = grad_ref[...], w_ref[...]
    grad = grad.reshape(-1, grad.shape[-1])
    total = dot_tn(grad, weight.reshape(-1, weight.shape[-1])).astype(jnp.bfloat16)
    half = ta_ref.shape[0]
    ta_ref[...] = total[:half]
    tb_ref[...] = total[half:]


def other_gradient(slot, info, rows, w_ref, hg_ref):
    expert, core, base, replica = info[slot], info[2], info[4], info[5]
    units, width = w_ref.shape[2:]
    rows, ids = split_rows(rows, width)
    select = select_rows(ids, base + expert, core, info[6])
    projected = dot_nt(w_ref[...].reshape(2 * units, width), rows)
    gate, up = projected[:units], projected[units:]
    grad = dot_nt(hg_ref[...], select)
    _, grad_gate, grad_up = gradients(gate, up, grad)
    return jnp.where(replica == 0, grad_gate, grad_up).astype(jnp.bfloat16)


def first_other_kernel(slot, pieces, info, w_ref, hg_ref, grad_ref, rows_ref, buffer, sems):
    rows_ref[...] = take_pieces(pieces, buffer, sems)
    grad_ref[...] = other_gradient(slot, info, rows_ref[...], w_ref, hg_ref)


def other_kernel(slot, info, rows_ref, w_ref, hg_ref, grad_ref):
    grad_ref[...] = other_gradient(slot, info, rows_ref[...], w_ref, hg_ref)


def weight_gradient(own_ref, other_ref, own_rows, other_rows):
    return jnp.dot(
        own_ref[0, 0], own_rows[...], preferred_element_type=jnp.float32
    ) + jnp.dot(other_ref[...], other_rows[...], preferred_element_type=jnp.float32)


def moments(grad, first, second):
    first = beta_one * first.astype(jnp.float32) + (1.0 - beta_one) * grad
    second = beta_two * second.astype(jnp.float32) + (1.0 - beta_two) * grad * grad
    return first, second


def step_weights(weight, first, second):
    return weight.astype(jnp.float32) - step_size * first / (jnp.sqrt(second) + adam_eps)


def leaving_kernel(info, own, other, a, b, m_ref, v_ref, *out_refs):
    grad = weight_gradient(own, other, a, b)
    first, second = moments(grad, m_ref[0, 0], v_ref[0, 0])
    start = 0
    for first_ref, second_ref in zip(out_refs[0::2], out_refs[1::2]):
        stop = start + first_ref.shape[0]
        first_ref[...] = first[start:stop].astype(jnp.bfloat16)
        second_ref[...] = second[start:stop].astype(jnp.bfloat16)
        start = stop


def staying_kernel(info, own, other, a, b, m_ref, v_ref, w_ref, nw_ref, nm_ref, nv_ref):
    grad = weight_gradient(own, other, a, b)
    first, second = moments(grad, m_ref[0, 0], v_ref[0, 0])
    nw_ref[0, 0] = step_weights(w_ref[0, 0], first, second).astype(jnp.bfloat16)
    nm_ref[0, 0] = first.astype(jnp.bfloat16)
    nv_ref[0, 0] = second.astype(jnp.bfloat16)


def arriving_kernel(info, _w, _m, _v, w_ref, m_ref, v_ref, nw_ref, nm_ref, nv_ref):
    height, span = 16, 1024
    for start in range(0, w_ref.shape[0], height):
        for left in range(0, w_ref.shape[1], span):
            at = (pl.ds(start, height), pl.ds(left, span))
            first, second = m_ref[at], v_ref[at]
            nw_ref[(0, 0, *at)] = step_weights(
                w_ref[at], first.astype(jnp.float32), second.astype(jnp.float32)
            ).astype(jnp.bfloat16)
            nm_ref[(0, 0, *at)] = first
            nv_ref[(0, 0, *at)] = second


def call(
    kernel,
    grid,
    in_specs,
    out_specs,
    out_shape,
    flops,
    moved,
    scratch=(),
    grant=VMEM_GRANT,
    **extra,
):
    def run(*args):
        return pl.pallas_call(
            kernel,
            grid_spec=pltpu.PrefetchScalarGridSpec(
                num_scalar_prefetch=1,
                grid=grid,
                in_specs=in_specs,
                out_specs=out_specs,
                scratch_shapes=scratch,
            ),
            out_shape=out_shape,
            compiler_params=pltpu.CompilerParams(vmem_limit_bytes=grant),
            cost_estimate=pl.CostEstimate(
                flops=flops, bytes_accessed=moved, transcendentals=0
            ),
            **extra,
        )(*args)

    return run


LEAVE, STAY = 0, 1


def fast_shards(tokens, expert_ids, weights, first_moment, second_moment, hidden_grad, swap_list):
    owners = lax.axis_size(EXPERT)
    row_count, width = tokens.shape
    _, per_dev, hidden_units, _ = hidden_grad.shape
    chips = owners // 2
    bf16, f32 = jnp.bfloat16, jnp.float32
    replica = lax.axis_index(DP)
    own_index = lax.axis_index(EXPERT)
    quarter = lax.axis_index(TENSOR)
    chosen, _ = migration_slot(swap_list, per_dev)
    core, chip, base = own_index % 2, own_index // 2, own_index * per_dev
    info = jnp.stack([chosen, 1 - chosen, core, chip, base, replica, quarter]).astype(jnp.int32)

    ids = jnp.pad(
        expert_ids.astype(bf16), ((0, 0), (0, IDS_COLS - expert_ids.shape[1])), constant_values=-1
    )
    rows = jnp.concatenate([tokens, ids], axis=1)
    sizes = (hidden_units // 3,) * 3
    starts = tuple(p * sizes[0] for p in range(3))

    def grad_slice(expert):
        return lax.dynamic_index_in_dim(hidden_grad[0], expert, 0, keepdims=False)

    leave_grad, stay_grad = grad_slice(chosen), grad_slice(1 - chosen)
    leave_weight = [
        lax.dynamic_slice(weights, (replica, chosen, start, 0), (1, 1, size, width))[0, 0]
        for start, size in zip(starts, sizes)
    ]

    half = row_count // 2
    low = lax.dynamic_slice_in_dim(rows, quarter * half, half, 0)
    low = flip(low, DP, 1)
    high = flip(low, TENSOR, 1)
    early = (info, stay_grad, leave_grad, *leave_weight)
    own_pieces = gather_plane([gather_chips(rows, early=early)])
    other_pieces = gather_plane([gather_chips(low), gather_chips(high, direct=True)])

    leave_other = flip(after(leave_grad, low), DP, 1)
    stay_other = flip(after(stay_grad, leave_other), DP, 1)
    gates = (own_pieces[2][0], other_pieces[2][0], other_pieces[3][1])
    weight_parts = [
        flip(after(piece, gate), EXPERT, Y_BIT)
        for piece, gate in zip(leave_weight, gates)
    ]

    wide = rows.shape[1]
    at_chip = lambda k, info: jnp.bitwise_xor(info[3], k)
    pair = 2 * row_count
    flat_rows = chips * pair
    matmul = 2 * per_dev * hidden_units * width * flat_rows * 2
    once = pl.Buffered(1)
    any_spec = pl.BlockSpec(memory_space=pl.ANY)
    rows_spec = pl.BlockSpec((pair, wide), lambda k, info: (k, 0))
    rows_shape = jax.ShapeDtypeStruct((flat_rows, wide), bf16)

    def piece_call(kernel, pieces, in_specs, out_specs, out_shape, flops):
        count = len(pieces[0])

        def body(info, *refs):
            grid = [list(refs[i * count : (i + 1) * count]) for i in range(chips)]
            kernel(grid, info, *refs[chips * count :])

        run = call(
            body,
            (chips,),
            [any_spec] * (chips * count) + in_specs,
            out_specs + [rows_spec],
            out_shape + [rows_shape],
            flops,
            20 << 20,
            [pltpu.VMEM((2, pair, wide), bf16), pltpu.SemaphoreType.DMA((2, count))],
        )
        return lambda info, *args: run(info, *[p for group in pieces for p in group], *args)

    slot_spec = pl.BlockSpec(
        (1, per_dev, hidden_units, pair), lambda k, info: (0, 0, 0, at_chip(k, info))
    )
    weight_spec = pl.BlockSpec(weights.shape, lambda k, info: (0, 0, 0, 0), pipeline_mode=once)
    own_grad_spec = pl.BlockSpec(
        (2, per_dev, hidden_units, pair), lambda k, info: (0, 0, 0, k)
    )
    hidden, own_grad, own_rows = piece_call(
        own_kernel,
        own_pieces,
        [weight_spec, slot_spec],
        [slot_spec, own_grad_spec],
        [
            jax.ShapeDtypeStruct(hidden_grad.shape, bf16),
            jax.ShapeDtypeStruct((2, per_dev, hidden_units, flat_rows), bf16),
        ],
        matmul,
    )(info, weights, hidden_grad)

    def other_specs(slot):
        return [
            pl.BlockSpec(
                (2, 1, hidden_units, width),
                lambda k, info: (0, info[slot], 0, 0),
                pipeline_mode=once,
            ),
            pl.BlockSpec((hidden_units, pair), lambda k, info: (0, at_chip(k, info))),
        ]

    other_out = pl.BlockSpec((hidden_units, pair), lambda k, info: (0, k))
    other_shape = jax.ShapeDtypeStruct((hidden_units, flat_rows), bf16)
    leave_terms, other_rows = piece_call(
        lambda *refs: first_other_kernel(LEAVE, *refs),
        other_pieces,
        other_specs(LEAVE),
        [other_out],
        [other_shape],
        matmul // 2,
    )(info, weights, leave_other)
    stay_terms = call(
        lambda *refs: other_kernel(STAY, *refs),
        (chips,),
        [rows_spec] + other_specs(STAY),
        other_out,
        other_shape,
        matmul // 2,
        9 << 20,
    )(info, other_rows, weights, stay_other)

    tile = 512
    tiles = width // tile
    flat_spec = pl.BlockSpec((flat_rows, tile), lambda j, info: (0, j))

    def update(slot, kernel, grad, states, out_specs, out_shapes):
        spec_at = lambda lead: pl.BlockSpec(
            (1, 1, hidden_units, tile), lambda j, info: (lead(info), info[slot], 0, j)
        )
        state_spec, half_spec = spec_at(lambda info: 0), spec_at(lambda info: info[5])
        specs = [
            pl.BlockSpec(
                (1, 1, hidden_units, flat_rows),
                lambda j, info: (info[5], info[slot], 0, 0),
                pipeline_mode=once,
            ),
            pl.BlockSpec((hidden_units, flat_rows), lambda j, info: (0, 0), pipeline_mode=once),
            flat_spec,
            flat_spec,
            state_spec,
            state_spec,
            half_spec,
        ]
        return call(
            kernel,
            (tiles,),
            specs[: 4 + len(states)],
            out_specs or [state_spec] * len(out_shapes),
            out_shapes,
            matmul // 2,
            18 << 20,
            grant=VMEM_GRANT if slot == LEAVE else STAY_GRANT,
        )(info, own_grad, grad, own_rows, other_rows, *states)

    sent = update(
        LEAVE,
        leaving_kernel,
        leave_terms,
        (first_moment, second_moment),
        [pl.BlockSpec((n, tile), lambda j, info: (0, j)) for n in sizes for _ in range(2)],
        [jax.ShapeDtypeStruct((n, width), bf16) for n in sizes for _ in range(2)],
    )
    first_in, second_in = [], []
    for p in range(len(sizes)):
        pair_out = sent[2 * p : 2 * p + 2]
        if p > 1:
            pair_out = [after(piece, second_in[0]) for piece in pair_out]
        first_in.append(flip(pair_out[0], EXPERT, Y_BIT))
        second_in.append(flip(pair_out[1], EXPERT, Y_BIT))

    half_spec = pl.BlockSpec((row_count, width), lambda k, info: (k, 0))
    ta, tb = call(
        token_kernel,
        (chips,),
        [own_grad_spec, weight_spec],
        [half_spec] * 2,
        [jax.ShapeDtypeStruct((flat_rows // 2, width), bf16)] * 2,
        matmul,
        20 << 20,
    )(info, own_grad, weights)

    def pick(value, index):
        return lax.dynamic_index_in_dim(value, index, value.ndim - 3, keepdims=False)

    def send(value, axis, bit):
        return flip(value.astype(bf16), axis, bit).astype(f32)

    core_sum = ta.astype(f32) + flip(tb, EXPERT, CORE).astype(f32)
    core_sum = core_sum.reshape(2, 2, 2, row_count // 2, width)
    sum_x, sum_z = core_sum[..., : width // 2], core_sum[..., width // 2 :]
    got_x = send(sum_x[:, 1], EXPERT, X_BIT)
    got_z = send(pick(sum_z, 1 - quarter), TENSOR, 1)
    sum_x = sum_x[:, 0] + got_x
    sum_z = pick(sum_z, quarter) + got_z
    sum_x = pick(sum_x, quarter) + send(pick(sum_x, 1 - quarter), TENSOR, 1)
    sum_z = sum_z[:, 0] + send(sum_z[:, 1], EXPERT, X_BIT)
    total = jnp.concatenate([sum_x, sum_z], axis=-1)
    token_grad = (total[0] + send(total[1], EXPERT, Y_BIT)).astype(bf16)

    state_shape = jax.ShapeDtypeStruct(first_moment.shape, bf16)
    stay_states = update(
        STAY,
        staying_kernel,
        stay_terms,
        (first_moment, second_moment, weights),
        None,
        [state_shape] * 3,
    )

    step_units = hidden_units // 6
    in_spec = pl.BlockSpec((step_units, width), lambda i, info: (i, 0))
    states = stay_states
    weight_parts[-1] = after(weight_parts[-1], token_grad)
    for p, (start, size) in enumerate(zip(starts, sizes)):
        out_spec = pl.BlockSpec(
            (1, 1, step_units, width),
            lambda i, info, first=start // step_units: (0, info[0], first + i, 0),
        )
        states = call(
            arriving_kernel,
            (size // step_units,),
            [any_spec] * 3 + [in_spec] * 3,
            [out_spec] * 3,
            [state_shape] * 3,
            0,
            5 << 20,
            input_output_aliases={1: 0, 2: 1, 3: 2},
        )(info, *states, weight_parts[p], first_in[p], second_in[p])
    return (hidden, token_grad, *states)


def token_layout_fits(tokens, expert_ids, weights, first, second, hidden_grad, swap_list):
    owners, parts = lax.axis_size(EXPERT), lax.axis_size(TENSOR)
    return (
        lax.axis_size(DP) == 2
        and owners == 8
        and parts == 2
        and weights.shape[1] == 2
        and 2 * swap_list.shape[0] == owners
        and tokens.shape[0] == 128
        and hidden_grad.shape[3] == owners * tokens.shape[0]
        and weights.shape[2] % 384 == 0
        and tokens.shape[1] % 256 == 0
    )


def plan(*args):
    if not token_layout_fits(*args):
        return shards(*args)
    return fast_shards(*args)


def solution(mesh):
    in_specs = (
        P((DP, EXPERT), None),
        P((DP, EXPERT), None),
        P(None, EXPERT, TENSOR, None),
        P(DP, EXPERT, TENSOR, None),
        P(DP, EXPERT, TENSOR, None),
        P(DP, EXPERT, TENSOR, None),
        P(),
    )
    out_specs = (
        P(DP, EXPERT, TENSOR, None),
        P((DP, EXPERT, TENSOR), None),
        P(DP, EXPERT, TENSOR, None),
        P(DP, EXPERT, TENSOR, None),
        P(DP, EXPERT, TENSOR, None),
    )
    return jax.shard_map(plan, mesh=mesh, in_specs=in_specs, out_specs=out_specs, check_vma=False)
```
